128 devices in a mesh: grp: 2 (over z_lo), row: 64 (over z_hi, x, y, core).
Axes of the slice: x: 4, y: 4, z: 4 (z_hi: 2, z_lo: 2; z = z_hi * 2 + z_lo), core: 2. Of those that a mesh axis runs over, the one named last changes fastest.
Arguments:
- inputs: bfloat16 [16384, 512], P('row'), may hold values from -6 to 6
- labels: int32 [16384], P('row'), may hold values from 0 to 999
- frequencies: float32 [512, 3072], P(None, 'grp'), may hold values from -0.25 to 0.25
- phases: float32 [3072], P('grp'), may hold values from 0 to 6.2832
- weights: float32 [3072, 1000], P('grp'), may hold values from -6 to 6
Outputs:
- new_weights: float32 [3072, 1000], P('grp')
- new_residual: float32 [16384, 1000], P('row')
The draws below stay inside these ranges and needn't reach their ends.
All inputs are finite; a program needn't handle non-finite values.
Results may differ from the reference program's by a relative error of at most 0.011.
Values sent between devices are 32-bit elements; how exact they have to be, the bound alone decides.
A program may use at most 192 MiB of HBM per device.

```python
import jax
import jax.numpy as jnp
from jax import lax

F = 1536
C = 1000
DIN = 512
GROUPS = 2
ROWS = 16384


def touch_ends(values, key, smallest, high):
    dims = values.shape
    spot = [jax.random.randint(jax.random.fold_in(key, axis), (), 0, dims[axis]) for axis in range(len(dims))]
    values = values.at[tuple(spot)].set(smallest)
    longest = dims.index(max(dims))
    spot[longest] = (spot[longest] + 1) % dims[longest]
    return values.at[tuple(spot)].set(high)


def steps_of(own_key, shape, cuts, least, largest):
    level = 1.0
    for position, parts in cuts:
        steps = jax.random.uniform(jax.random.fold_in(jax.random.fold_in(own_key, 6), position), (parts,), jnp.float32, least / len(cuts), largest / len(cuts))
        level = level * jnp.repeat(jnp.exp(steps), shape[position] // parts).reshape((-1,) + (1,) * (len(shape) - 1 - position))
    return level


def normal_values(rng, shape, width, reach, shards=(), held_as=jnp.bfloat16):
    result = jax.random.normal(rng, shape, jnp.float32) * width
    if len(shards) > 0:
        result = steps_of(rng, shape, shards, -0.22, 0.18) * result
    return jnp.clip(result, min=-reach, max=reach).astype(held_as)


def setup_inputs(seed: int = 0) -> dict:
    streams_of = jax.random.split(jax.random.key(seed), 6)
    return {
        "inputs": normal_values(streams_of[0], (ROWS, DIN), 1.0, 6.0, ((0, 64),)),
        "labels": touch_ends(jax.random.randint(streams_of[1], (ROWS,), 0, C), jax.random.fold_in(streams_of[1], 1), 0, C - 1).astype(jnp.int32),
        "frequencies": normal_values(streams_of[2], (DIN, GROUPS * F), DIN ** -0.5, 0.25, ((1, 2),), jnp.float32),
        "phases": jnp.clip(6.2832 * jax.random.uniform(streams_of[3], (GROUPS * F,), jnp.float32) ** steps_of(streams_of[3], (GROUPS * F,), ((0, 2),), -0.2, 0.2), 0.0, 6.2832),
        "weights": normal_values(streams_of[4], (GROUPS * F, C), 1.0, 6.0, ((0, 2),), jnp.float32),
    }


RIDGE = 1.0
DAMP = 0.5

def reference(inputs, labels, frequencies, phases, weights):
    scale = (2.0 / (GROUPS * F)) ** 0.5
    onehot = (labels[:, None] == jnp.arange(C, dtype=jnp.int32)[None, :]).astype(jnp.float32)
    feats = []
    prediction = jnp.zeros((ROWS, C), jnp.float32)
    for group in range(GROUPS):
        low = group * F
        arg = jnp.dot(inputs.astype(jnp.float32), frequencies[:, low:low + F], precision=lax.Precision.HIGHEST) + phases[low:low + F][None, :]
        phi = (scale * jnp.cos(arg)).astype(jnp.bfloat16)
        feats.append(phi)
        prediction = prediction + jnp.dot(phi.astype(jnp.float32), weights[low:low + F].astype(jnp.bfloat16).astype(jnp.float32), preferred_element_type=jnp.float32)
    residual = onehot - prediction
    res_low = residual.astype(jnp.bfloat16)
    updated = []
    change = jnp.zeros((ROWS, C), jnp.float32)
    for group in range(GROUPS):
        low = group * F
        phi = feats[group]
        gram = jnp.dot(phi.T.astype(jnp.float32), phi.astype(jnp.float32), preferred_element_type=jnp.float32)
        rhs = jnp.dot(phi.T.astype(jnp.float32), res_low.astype(jnp.float32), preferred_element_type=jnp.float32) - RIDGE * weights[low:low + F]
        system = gram + RIDGE * jnp.eye(F, dtype=jnp.float32)
        factor = jnp.linalg.cholesky(system)
        solution = jax.scipy.linalg.cho_solve((factor, True), rhs)
        step = DAMP * solution
        updated.append(weights[low:low + F] + step)
        change = change + jnp.dot(phi.astype(jnp.float32), step.astype(jnp.bfloat16).astype(jnp.float32), preferred_element_type=jnp.float32)
    return (jnp.concatenate(updated, axis=0), residual - change)
```

```python
import functools

import jax
import jax.numpy as jnp
from jax import lax
from jax.experimental import pallas as pl
from jax.experimental.pallas import tpu as pltpu
from jax.sharding import PartitionSpec as P

RIDGE = 1.0
DAMP = 0.5
MESH = pl.DeviceIdType.MESH
B = 128
VMEM_LIMIT = 62 * 1024 * 1024

CORE, XA, XB, YA, YB, ZH = range(6)
ORDERS = (
    (CORE, XA, XB, YA, YB, ZH),
    (CORE, YA, YB, XA, XB, ZH),
    (CORE, XB, XA, YB, YA, ZH),
    (CORE, YB, YA, XB, XA, ZH),
)
COLORS = len(ORDERS)
STAGES = 6


def place():
    r = lax.axis_index("row")
    core, y, x, z = lax.rem(r, 2), lax.rem(r // 2, 4), lax.rem(r // 8, 4), r // 32
    at = lambda z, x, y, core: ((z * 4 + x) * 4 + y) * 2 + core
    flip = lambda q: q + 1 - 2 * lax.rem(q, 2)
    bits = (core, lax.rem((x + 1) // 2, 2), x // 2, lax.rem((y + 1) // 2, 2), y // 2, z)
    partners = (
        at(z, x, y, 1 - core),
        at(z, flip(x), y, core),
        at(z, 3 - x, y, core),
        at(z, x, flip(y), core),
        at(z, x, 3 - y, core),
        at(1 - z, x, y, core),
    )
    return bits, partners


def meet(partners):
    barrier = pltpu.get_barrier_semaphore()
    for partner in partners:
        pl.semaphore_signal(barrier, inc=1, device_id={"row": partner}, device_id_type=MESH)
    pl.semaphore_wait(barrier, len(partners))


def send(src, dst, send_sem, recv_sem, partner):
    copy = pltpu.make_async_remote_copy(
        src_ref=src,
        dst_ref=dst,
        send_sem=send_sem,
        recv_sem=recv_sem,
        device_id={"row": partner},
        device_id_type=MESH,
    )
    copy.start()
    return copy


def packed_offsets(n):
    return [sum(n - B * i for i in range(j)) for j in range(n // B + 1)]


def packed_rows(n):
    return -(-packed_offsets(n)[-1] // 2048) * 2048


def gram_kernel(phi_ref, out_ref, phit, part, acc, land, rs_s, rs_r, ag_s, ag_r):
    bits, partners = place()
    n = phi_ref.shape[1]
    offsets = packed_offsets(n)
    total = out_ref.shape[0]
    for j in range(n // B):
        phit[B * j : B * j + B, :] = phi_ref[:, B * j : B * j + B].T
    for j in range(n // B):
        part[offsets[j] : offsets[j + 1], :] = lax.dot_general(
            phit[B * j :, :],
            phit[B * j : B * j + B, :],
            (((1,), (1,)), ((), ())),
            preferred_element_type=jnp.float32,
        )
    part[offsets[-1] :, :] = jnp.zeros((total - offsets[-1], B), jnp.float32)
    meet(partners)
    span = total // COLORS
    low = [jnp.int32(span * c) for c in range(COLORS)]

    def reduce_start(c, s, src):
        size = span >> (s + 1)
        axis = ORDERS[c][s]
        give = pl.multiple_of(low[c] + (1 - bits[axis]) * size, 8)
        low[c] = low[c] + bits[axis] * size
        base = span * c + (span - (span >> s))
        return send(
            src.at[pl.ds(give, size), :],
            land.at[pl.ds(base, size), :],
            rs_s.at[c, s],
            rs_r.at[c, s],
            partners[axis],
        )

    def gather_start(c, s):
        size = span >> (s + 1)
        axis = ORDERS[c][s]
        mine = pl.ds(pl.multiple_of(low[c], 8), size)
        low[c] = low[c] - bits[axis] * size
        return send(
            out_ref.at[mine, :], out_ref.at[mine, :], ag_s.at[c, s], ag_r.at[c, s], partners[axis]
        )

    pending = [reduce_start(c, 0, part) for c in range(COLORS)]
    for s in range(STAGES):
        size = span >> (s + 1)
        have = part if s == 0 else acc
        to = out_ref if s == STAGES - 1 else acc
        rows = min(size, 320)
        for c in range(COLORS):
            pending[c].wait()
            base = span * c + (span - (span >> s))
            here = low[c]

            @pl.loop(0, size // rows)
            def _(i):
                q = pl.ds(pl.multiple_of(here + i * rows, 8), rows)
                to[q, :] = have[q, :] + land[pl.ds(pl.multiple_of(base + i * rows, 8), rows), :]

            pending[c] = reduce_start(c, s + 1, acc) if s < STAGES - 1 else gather_start(c, s)
    for s in range(STAGES - 1, -1, -1):
        for c in range(COLORS):
            pending[c].wait()
            if s:
                pending[c] = gather_start(c, s - 1)


def gram_of_all_rows(phi):
    rows, n = phi.shape
    total = packed_rows(n)
    vmem = pl.BlockSpec(memory_space=pltpu.VMEM)
    return pl.pallas_call(
        gram_kernel,
        out_shape=jax.ShapeDtypeStruct((total, B), jnp.float32),
        in_specs=[vmem],
        out_specs=vmem,
        scratch_shapes=[pltpu.VMEM((n, rows), jnp.bfloat16)]
        + [pltpu.VMEM((total, B), jnp.float32)] * 3
        + [pltpu.SemaphoreType.DMA((COLORS, STAGES))] * 4,
        compiler_params=pltpu.CompilerParams(
            vmem_limit_bytes=VMEM_LIMIT, collective_id=0, has_side_effects=True
        ),
        cost_estimate=pl.CostEstimate(
            flops=2 * rows * n * n, bytes_accessed=150_000_000, transcendentals=0
        ),
        name="gram_of_all_rows",
    )(phi)


def split(v):
    high = v.astype(jnp.bfloat16)
    return high, (v - high.astype(jnp.float32)).astype(jnp.bfloat16)


def dot3(ah, al, bh, bl, dims):
    dot = functools.partial(
        lax.dot_general, dimension_numbers=(dims, ((), ())), preferred_element_type=jnp.float32
    )
    return dot(ah, bh) + (dot(ah, bl) + dot(al, bh))


def sweep8(strips):
    tile = (8, B)
    lane = lax.broadcasted_iota(jnp.int32, tile, 1)
    sub = lax.broadcasted_iota(jnp.int32, tile, 0)
    top = strips[0]
    row = lambda v, p: jnp.broadcast_to(v[p : p + 1, :], tile)
    column = lambda v, p: jnp.broadcast_to(v[:, p : p + 1], tile)
    key = lambda i, j: (i, j) if i >= j else (j, i)
    a = {}
    for q in range(8):
        col = column(top, q)
        for p in range(q, 8):
            a[p, q] = row(col, p)
    for p in range(8):
        inv = 1.0 / a[p, p]
        scaled = {i: a[key(i, p)] * inv for i in range(8) if i != p}
        for i in range(8):
            for j in range(i + 1):
                if i != p and j != p:
                    a[i, j] = a[i, j] - scaled[i] * a[key(j, p)]
        for i in scaled:
            a[key(i, p)] = scaled[i]
        a[p, p] = -inv
    held = jnp.where(lane < 8, jnp.where(lane == sub, -1.0, 0.0), top)
    rows = [row(held, q) for q in range(8)]
    swept = []
    for p in range(8):
        t = [a[key(p, q)] * rows[q] for q in range(8)]
        swept.append(((t[0] + t[1]) + (t[2] + t[3])) + ((t[4] + t[5]) + (t[6] + t[7])))
    out = []
    for v in strips[1:]:
        w = jnp.where(lane < 8, 0.0, v)
        for p in range(8):
            w = w + column(v, p) * swept[p]
        out.append(w)
    first = swept[0]
    for p in range(1, 8):
        first = jnp.where(sub == p, swept[p], first)
    out.append(-first)
    return tuple(pltpu.roll(v, B - 8, 1) for v in out)


def inverse(block):
    strips = tuple(block[8 * i : 8 * i + 8, :] for i in range(B // 8))
    strips = lax.fori_loop(0, B // 8, lambda _, held: sweep8(held), strips)
    return -jnp.concatenate(strips, axis=0)


def solve_kernel(
    gram_ref, phi_ref, res_ref, own_ref, out_ref, part, land, wh, wl, sh, sl, yh, yl, rs_s, rs_r, ag_s, ag_r
):
    bits, partners = place()
    n = phi_ref.shape[1]
    count = n // B
    offsets = packed_offsets(n)
    per = out_ref.shape[6]
    lanes = n // COLORS

    for i in range(2):
        for k in range(4):
            part[i, k // 2, k % 2] = lax.dot_general(
                res_ref[pl.ds((i * 4 + k) * 8 * per, 8 * per), :],
                phi_ref[...],
                (((1,), (0,)), ((), ())),
                preferred_element_type=jnp.float32,
            ).reshape(2, 2, 2, per, n)
    meet(partners)

    def index(c, s, value):
        where = [slice(None)] * STAGES
        for axis in ORDERS[c][:s]:
            where[axis] = bits[axis]
        where[ORDERS[c][s]] = value
        return tuple(where) + (slice(None), pl.ds(lanes * c, lanes))

    def reduce_start(c, s):
        axis = ORDERS[c][s]
        return send(
            part.at[index(c, s, 1 - bits[axis])],
            land.at[index(c, s, bits[axis])],
            rs_s.at[c, s],
            rs_r.at[c, s],
            partners[axis],
        )

    def reduce_add(c, s):
        axis = ORDERS[c][s]
        mine = index(c, s, bits[axis])
        theirs = index(c, s, 1 - bits[axis])
        part[mine] = part[mine] + land[theirs]

    def gather_start(c, s):
        mine = index(c, s, bits[ORDERS[c][s]])
        return send(
            out_ref.at[mine],
            out_ref.at[mine],
            ag_s.at[c, s],
            ag_r.at[c, s],
            partners[ORDERS[c][s]],
        )

    pending = [reduce_start(c, 0) for c in range(COLORS)]
    stage_before = {2: 0, 4: 1, 6: 2, 7: 3, 8: 4, 9: 5}

    eye = (
        lax.broadcasted_iota(jnp.int32, (B, B), 0) == lax.broadcasted_iota(jnp.int32, (B, B), 1)
    ).astype(jnp.float32)
    inverses = []
    for j in range(count):
        if j in stage_before:
            s = stage_before[j]
            for c in range(COLORS):
                pending[c].wait()
                reduce_add(c, s)
                if s < STAGES - 1:
                    pending[c] = reduce_start(c, s + 1)
        width = B * j
        start = B * j

        def updated(t):
            v = gram_ref[pl.ds(pl.multiple_of(offsets[j] - start + t * B, B), B), :]
            if j:
                at = pl.ds(pl.multiple_of(t * B, B), B)
                v = v - dot3(
                    wh[at, :width],
                    wl[at, :width],
                    sh[start : start + B, :width],
                    sl[start : start + B, :width],
                    ((1,), (1,)),
                )
            return v

        ih, il = split(inverse(updated(j) + RIDGE * eye))
        inverses.append((ih, il))
        wh[start : start + B, start : start + B] = ih
        wl[start : start + B, start : start + B] = il
        if j < count - 1:

            @pl.loop(j + 1, count)
            def _(t):
                at = pl.ds(pl.multiple_of(t * B, B), B)
                h, l = split(updated(t))
                sh[at, start : start + B] = h
                sl[at, start : start + B] = l
                h, l = split(dot3(h, l, ih, il, ((1,), (0,))))
                wh[at, start : start + B] = h
                wl[at, start : start + B] = l

    home = tuple(bits) + (slice(None), slice(None))
    rhs = part[home] - RIDGE * own_ref[...]
    for j in range(count):
        here = slice(B * j, B * j + B)
        y = rhs[:, here]
        if j:
            y = y - dot3(
                yh[:, : B * j], yl[:, : B * j], wh[here, : B * j], wl[here, : B * j], ((1,), (1,))
            )
        yh[:, here], yl[:, here] = split(y)
    for j in range(count - 1, -1, -1):
        here = slice(B * j, B * j + B)
        x = dot3(yh[:, here], yl[:, here], wh[here, here], wl[here, here], ((1,), (0,)))
        if j < count - 1:
            after = slice(B * j + B, n)
            x = x - dot3(yh[:, after], yl[:, after], wh[after, here], wl[after, here], ((1,), (0,)))
        out_ref[tuple(bits) + (slice(None), here)] = x
        yh[:, here], yl[:, here] = split(x)
    pending = [gather_start(c, STAGES - 1) for c in range(COLORS)]
    for s in range(STAGES - 1, -1, -1):
        for c in range(COLORS):
            pending[c].wait()
            if s:
                pending[c] = gather_start(c, s - 1)


def solution_of_all_classes(gram, phi, res, own):
    rows, n = phi.shape
    padded = res.shape[0]
    per = padded >> STAGES
    blocks = (2,) * STAGES + (per, n)
    vmem = pl.BlockSpec(memory_space=pltpu.VMEM)
    out = pl.pallas_call(
        solve_kernel,
        out_shape=jax.ShapeDtypeStruct(blocks, jnp.float32),
        in_specs=[vmem] * 4,
        out_specs=vmem,
        scratch_shapes=[pltpu.VMEM(blocks, jnp.float32)] * 2
        + [pltpu.VMEM((n, n), jnp.bfloat16)] * 4
        + [pltpu.VMEM((per, n), jnp.bfloat16)] * 2
        + [pltpu.SemaphoreType.DMA((COLORS, STAGES))] * 4,
        compiler_params=pltpu.CompilerParams(
            vmem_limit_bytes=VMEM_LIMIT, collective_id=1, has_side_effects=True
        ),
        cost_estimate=pl.CostEstimate(
            flops=2 * n * n * n, bytes_accessed=300_000_000, transcendentals=0
        ),
        name="solution_of_all_classes",
    )(gram, phi, res, own)
    return out.reshape(padded, n)


def body(inputs, labels, frequencies, phases, weights):
    groups = lax.axis_size("grp")
    width = frequencies.shape[1]
    classes = weights.shape[1]
    padded = -(-classes // 1024) * 1024
    scale = (2.0 / (groups * width)) ** 0.5
    swap = [(0, 1), (1, 0)]
    arg = (
        jnp.dot(inputs.astype(jnp.float32), frequencies, precision=lax.Precision.HIGHEST)
        + phases[None, :]
    )
    phi = (scale * jnp.cos(arg)).astype(jnp.bfloat16)
    onehot = (labels[:, None] == lax.broadcasted_iota(jnp.int32, (1, classes), 1)).astype(
        jnp.float32
    )
    own = jnp.dot(phi, weights.astype(jnp.bfloat16), preferred_element_type=jnp.float32)
    other = lax.ppermute(own, "grp", swap)
    gram = gram_of_all_rows(phi)
    residual = onehot - (own + other)
    res_low = jnp.pad(residual.astype(jnp.bfloat16).T, ((0, padded - classes), (0, 0)))

    bits, _ = place()
    piece = 0
    for bit in bits:
        piece = piece * 2 + bit
    per = padded // 64
    start = jnp.minimum(piece * per, classes - per)
    beyond = piece * per - start
    kept = lax.dynamic_slice(weights, (0, start), (width, per)).T
    own_weights = jnp.zeros_like(kept)
    for shift in sorted({max(0, p * per - (classes - per)) for p in range(64)}):
        if shift < per:
            moved = jnp.pad(kept[shift:, :], ((0, shift), (0, 0)))
            own_weights = jnp.where(beyond == shift, moved, own_weights)

    solution = solution_of_all_classes(gram, phi, res_low, own_weights)[:classes]
    step = DAMP * solution
    delta = lax.dot_general(
        phi, step.astype(jnp.bfloat16), (((1,), (1,)), ((), ())), preferred_element_type=jnp.float32
    )
    change = delta + lax.ppermute(delta, "grp", swap)
    return (weights + step.T, residual - change)


def solution(mesh):
    return jax.shard_map(
        body,
        mesh=mesh,
        in_specs=(P("row", None), P("row"), P(None, "grp"), P("grp"), P("grp", None)),
        out_specs=(P("grp", None), P("row", None)),
        check_vma=False,
    )
```

```python
import functools

import jax
import jax.numpy as jnp
from jax import lax
from jax.experimental import pallas as pl
from jax.experimental.pallas import tpu as pltpu
from jax.sharding import PartitionSpec as P

RIDGE = 1.0
DAMP = 0.5
MESH = pl.DeviceIdType.MESH
B = 128
VMEM_LIMIT = 62 * 1024 * 1024

CORE, XA, XB, YA, YB, ZH = range(6)
ORDERS = (
    (CORE, XA, XB, YA, YB, ZH),
    (CORE, YA, YB, XA, XB, ZH),
    (CORE, XB, XA, YB, YA, ZH),
    (CORE, YB, YA, XB, XA, ZH),
)
COLORS = len(ORDERS)
STAGES = 6


def place():
    r = lax.axis_index("row")
    core, y, x, z = lax.rem(r, 2), lax.rem(r // 2, 4), lax.rem(r // 8, 4), r // 32
    at = lambda z, x, y, core: ((z * 4 + x) * 4 + y) * 2 + core
    flip = lambda q: q + 1 - 2 * lax.rem(q, 2)
    bits = (core, lax.rem((x + 1) // 2, 2), x // 2, lax.rem((y + 1) // 2, 2), y // 2, z)
    partners = (
        at(z, x, y, 1 - core),
        at(z, flip(x), y, core),
        at(z, 3 - x, y, core),
        at(z, x, flip(y), core),
        at(z, x, 3 - y, core),
        at(1 - z, x, y, core),
    )
    return bits, partners


def send(src, dst, send_sem, recv_sem, partner):
    copy = pltpu.make_async_remote_copy(
        src_ref=src,
        dst_ref=dst,
        send_sem=send_sem,
        recv_sem=recv_sem,
        device_id={"row": partner},
        device_id_type=MESH,
    )
    copy.start()
    return copy


def packed_offsets(n):
    return [sum(n - B * i for i in range(j)) for j in range(n // B + 1)]


def packed_rows(n):
    return -(-packed_offsets(n)[-1] // 2048) * 2048


def pieces(v):
    high = v.astype(jnp.bfloat16)
    rest = v - high.astype(jnp.float32)
    middle = rest.astype(jnp.bfloat16)
    return high, middle, (rest - middle.astype(jnp.float32)).astype(jnp.bfloat16)


def dot32(stack, right, dims):
    m = stack.shape[0] // 3
    dot = functools.partial(
        lax.dot_general, dimension_numbers=(dims, ((), ())), preferred_element_type=jnp.float32
    )
    high, middle, low = dot(stack, right[0]), dot(stack[: 2 * m], right[1]), dot(stack[:m], right[2])
    return high[:m] + ((high[m : 2 * m] + middle[:m]) + (high[2 * m :] + middle[m:] + low))


def stacked(v):
    return jnp.concatenate(pieces(v), axis=0)


def tree(t):
    return ((t[0] + t[1]) + (t[2] + t[3])) + ((t[4] + t[5]) + (t[6] + t[7]))


def key(i, j):
    return (i, j) if i >= j else (j, i)


def inverse8(a):
    for p in range(0, 8, 2):
        q = p + 1
        first, cross, second = a[p, p], a[q, p], a[q, q]
        det = first * second - cross * cross
        r = pl.reciprocal(det, approx=True)
        r = r * (2.0 - det * r)
        r = r * (2.0 - det * r)
        e, f, h = second * r, -(cross * r), first * r
        others = [i for i in range(8) if i not in (p, q)]
        u = {i: a[key(i, p)] for i in others}
        v = {i: a[key(i, q)] for i in others}
        mu = {i: u[i] * e + v[i] * f for i in others}
        mv = {i: u[i] * f + v[i] * h for i in others}
        for i in others:
            for j in others:
                if j <= i:
                    a[i, j] = a[i, j] - (mu[i] * u[j] + mv[i] * v[j])
        for i in others:
            a[key(i, p)], a[key(i, q)] = mu[i], mv[i]
        a[p, p], a[q, p], a[q, q] = -e, -f, -h
    return a


def inverse(block, scratch, parts):
    d_ref, p_ref, q_ref, t_ref, s_ref = scratch
    tile = (8, B)
    lane = lax.broadcasted_iota(jnp.int32, tile, 1)
    sub = lax.broadcasted_iota(jnp.int32, tile, 0)
    lanes = lax.broadcasted_iota(jnp.int32, (B, B), 1)
    d_ref[...] = block
    p_ref[...] = jnp.zeros(p_ref.shape, p_ref.dtype)
    q_ref[...] = jnp.zeros(q_ref.shape, q_ref.dtype)
    t_ref[...] = jnp.zeros(tile, jnp.float32)

    def columns(v, k):
        return [
            jnp.take_along_axis(v, jnp.full(tile, k + q, jnp.int32), axis=1) for q in range(8)
        ]

    def late():
        return lax.dot_general(
            p_ref[...], q_ref[...], (((0,), (0,)), ((), ())), preferred_element_type=jnp.float32
        )

    def step(b, top, also):
        k = pl.multiple_of(b * 8, 8)
        was = pl.multiple_of(lax.rem(k + B - 8, B), 8)
        update = late()
        below = d_ref[pl.ds(pl.multiple_of(lax.rem(k + 8, B), 8), 8), :]
        before = jnp.logical_and(jnp.logical_and(lane >= was, lane < was + 8), k > 0)
        cols = columns(below, was)
        below = jnp.where(before, 0.0, below) + tree(
            [cols[p] * jnp.broadcast_to(t_ref[p : p + 1, :], tile) for p in range(8)]
        )
        for q, col in enumerate(columns(top, k)):
            s_ref[8 * q : 8 * q + 8, :] = col
        a = {}
        for q in range(8):
            for p in range(q, 8):
                a[p, q] = jnp.broadcast_to(s_ref[8 * q + p : 8 * q + p + 1, :], tile)
        a = inverse8(a)
        now = jnp.logical_and(lane >= k, lane < k + 8)
        s_ref[64:72, :] = jnp.where(now, jnp.where(lane - k == sub, -1.0, 0.0), top)
        rows = [jnp.broadcast_to(s_ref[64 + q : 65 + q, :], tile) for q in range(8)]
        swept = [tree([a[key(p, q)] * rows[q] for q in range(8)]) for p in range(8)]
        cols = columns(below, k)
        below = jnp.where(now, 0.0, below) + tree([cols[p] * swept[p] for p in range(8)])
        strip = swept[0]
        for p in range(1, 8):
            strip = jnp.where(sub == p, swept[p], strip)
        place = lanes - was
        done = jnp.logical_and(k > 0, jnp.logical_and(place >= 0, place < 8))
        d_ref[...] = jnp.where(done, 0.0, d_ref[...]) + update
        d_ref[pl.ds(was, 8), :] = jnp.where(k > 0, -t_ref[...], d_ref[pl.ds(was, 8), :])
        uh, um, ul = (v.astype(jnp.float32) for v in pieces(top))
        th, tm, tl = (v.astype(jnp.float32) for v in pieces(strip))
        p_ref[...] = jnp.concatenate([uh, uh, um, uh, um, ul], axis=0).astype(jnp.bfloat16)
        q_ref[...] = jnp.concatenate([th, tm, th, tl, tm, th], axis=0).astype(jnp.bfloat16)
        t_ref[...] = strip
        if also is not None:
            also(b)
        return below

    top = block[:8, :]
    begin = 0
    for steps, also, after in parts:
        if steps:
            top = lax.fori_loop(
                begin, begin + steps, lambda b, v, also=also: step(b, v, also), top
            )
        begin += steps
        after()
    d = jnp.where(lanes >= B - 8, 0.0, d_ref[...]) + late()
    return -jnp.concatenate([d[: B - 8, :], -t_ref[...]], axis=0)


def sweep_kernel(
    phi_ref, own_ref, label_ref, weight_ref,
    out_ref, res_ref,
    phit, gpart, gland, a_ref, rpart, rland, other, low_ref, lowt, w_ref, rs, dv, ys,
    d_ref, p_ref, q_ref, t_ref, s_ref,
    swap_sem, grs_s, grs_r, gag_s, gag_r, rs_s, rs_r, ag_s, ag_r,
):
    bits, partners = place()
    group = lax.axis_index("grp")
    n = phi_ref.shape[1]
    count = n // B
    offsets = packed_offsets(n)
    total = a_ref.shape[0]
    classes = own_ref.shape[1]
    per = out_ref.shape[6]
    lanes = n // COLORS
    block = lambda j: slice(B * j, B * j + B)

    for j in range(count):
        phit[block(j), :] = phi_ref[:, block(j)].T
    for j in range(count):
        gpart[offsets[j] : offsets[j + 1], :] = lax.dot_general(
            phit[B * j :, :],
            phit[block(j), :],
            (((1,), (1,)), ((), ())),
            preferred_element_type=jnp.float32,
        )
    gpart[offsets[-1] :, :] = jnp.zeros((total - offsets[-1], B), jnp.float32)

    barrier = pltpu.get_barrier_semaphore()
    pl.semaphore_signal(barrier, inc=1, device_id={"grp": 1 - group}, device_id_type=MESH)
    for partner in partners:
        pl.semaphore_signal(barrier, inc=1, device_id={"row": partner}, device_id_type=MESH)
    pl.semaphore_wait(barrier, len(partners) + 1)

    swap = pltpu.make_async_remote_copy(
        src_ref=own_ref,
        dst_ref=other,
        send_sem=swap_sem.at[0],
        recv_sem=swap_sem.at[1],
        device_id={"grp": 1 - group},
        device_id_type=MESH,
    )
    swap.start()

    def gram_wave(w, base, rows):
        span = rows // COLORS
        low = [jnp.int32(base + span * c) for c in range(COLORS)]

        def reduce_start(c, s, src):
            size = span >> (s + 1)
            axis = ORDERS[c][s]
            give = pl.multiple_of(low[c] + (1 - bits[axis]) * size, 8)
            low[c] = low[c] + bits[axis] * size
            land = base + span * c + (span - (span >> s))
            return send(
                src.at[pl.ds(give, size), :],
                gland.at[pl.ds(land, size), :],
                grs_s.at[w, c, s],
                grs_r.at[w, c, s],
                partners[axis],
            )

        def gather_start(c, s):
            size = span >> (s + 1)
            axis = ORDERS[c][s]
            mine = pl.ds(pl.multiple_of(low[c], 8), size)
            low[c] = low[c] - bits[axis] * size
            return send(
                a_ref.at[mine, :], a_ref.at[mine, :], gag_s.at[w, c, s], gag_r.at[w, c, s], partners[axis]
            )

        pending = [reduce_start(c, 0, gpart) for c in range(COLORS)]
        yield
        for s in range(STAGES):
            size = span >> (s + 1)
            to = a_ref if s == STAGES - 1 else gpart
            step = min(size, 256)
            for c in range(COLORS):
                pending[c].wait()
                land = base + span * c + (span - (span >> s))
                here = low[c]

                @pl.loop(0, size // step)
                def _(i):
                    q = pl.ds(pl.multiple_of(here + i * step, 8), step)
                    to[q, :] = gpart[q, :] + gland[pl.ds(pl.multiple_of(land + i * step, 8), step), :]

                pending[c] = reduce_start(c, s + 1, gpart) if s < STAGES - 1 else gather_start(c, s)
            yield
        for s in range(STAGES - 1, -1, -1):
            for c in range(COLORS):
                pending[c].wait()
                if s:
                    pending[c] = gather_start(c, s - 1)
            yield

    def index(c, s, value):
        where = [slice(None)] * STAGES
        for axis in ORDERS[c][:s]:
            where[axis] = bits[axis]
        where[ORDERS[c][s]] = value
        return tuple(where) + (slice(None), pl.ds(lanes * c, lanes))

    def rhs_sum():
        swap.wait()
        hot = label_ref[...] == lax.broadcasted_iota(jnp.int32, (1, classes), 1)
        residual = hot.astype(jnp.float32) - (own_ref[...] + other[...])
        res_ref[...] = residual
        low_ref[...] = jnp.zeros(low_ref.shape, low_ref.dtype)
        low_ref[:, :classes] = residual.astype(jnp.bfloat16)
        for i in range(lowt.shape[0] // B):
            lowt[block(i), :] = low_ref[:, block(i)].T
        for i in range(8):
            rpart[i // 4, i // 2 % 2, i % 2] = lax.dot_general(
                lowt[i * 8 * per : (i + 1) * 8 * per, :],
                phi_ref[...],
                (((1,), (0,)), ((), ())),
                preferred_element_type=jnp.float32,
            ).reshape(2, 2, 2, per, n)

        def start(c, s):
            axis = ORDERS[c][s]
            return send(
                rpart.at[index(c, s, 1 - bits[axis])],
                rland.at[index(c, s, bits[axis])],
                rs_s.at[c, s],
                rs_r.at[c, s],
                partners[axis],
            )

        pending = [start(c, 0) for c in range(COLORS)]
        yield
        for s in range(STAGES):
            for c in range(COLORS):
                pending[c].wait()
                mine = index(c, s, bits[ORDERS[c][s]])
                rpart[mine] = rpart[mine] + rland[index(c, s, 1 - bits[ORDERS[c][s]])]
                if s < STAGES - 1:
                    pending[c] = start(c, s + 1)
            yield

    waves = dict(
        A=gram_wave(0, 0, 2048),
        B=gram_wave(1, 2048, 4096),
        C=gram_wave(2, 6144, total - 6144),
        R=rhs_sum(),
    )

    def go(names):
        for name in names:
            next(waves[name], None)

    hooks = dict(HOOKS)

    scratch = (d_ref, p_ref, q_ref, t_ref, s_ref)
    eye = (
        lax.broadcasted_iota(jnp.int32, (B, B), 0) == lax.broadcasted_iota(jnp.int32, (B, B), 1)
    ).astype(jnp.float32)
    go(hooks["start"])
    system = a_ref[:B, :] + RIDGE * eye
    for j in range(count):
        go(hooks.get((j, 0), ""))
        here = block(j)
        width = B * j

        def row_of(t, j=j, here=here, width=width):
            at = pl.ds(pl.multiple_of(t * B, B), B)
            old = pl.ds(pl.multiple_of(offsets[j - 1] + (t - j + 1) * B, B), B)
            new = pl.ds(pl.multiple_of(offsets[j] + (t - j) * B, B), B)
            w_ref[at, block(j - 1)] = dot32(
                stacked(a_ref[old, :]), (dv[0], dv[1], dv[2]), ((1,), (0,))
            )
            a_ref[new, :] = a_ref[new, :] - dot32(
                stacked(w_ref[at, :width]), [rs[i, :, :width] for i in range(3)], ((1,), (1,))
            )

        with_rows = count - 1 - j if j else 0
        parts = [
            (with_rows, lambda b, j=j, f=row_of: f(j + 1 + b), lambda j=j: go(hooks.get((j, 1), ""))),
            (B // 8 - with_rows, None, lambda j=j: go(hooks.get((j, 2), ""))),
        ]
        inv = inverse(system, scratch, parts)
        w_ref[here, here] = inv
        if j < count - 1:
            dv[0], dv[1], dv[2] = pieces(inv)
            after = block(j + 1)
            w_ref[after, here] = dot32(
                stacked(a_ref[offsets[j] + B : offsets[j] + 2 * B, :]),
                (dv[0], dv[1], dv[2]),
                ((1,), (0,)),
            )
            for k in range(j + 1):
                at = offsets[k] + (j + 1 - k) * B
                rs[0, :, block(k)], rs[1, :, block(k)], rs[2, :, block(k)] = pieces(
                    a_ref[at : at + B, :]
                )
            width = B * (j + 1)
            system = (a_ref[offsets[j + 1] : offsets[j + 1] + B, :] + RIDGE * eye) - dot32(
                stacked(w_ref[after, :width]), [rs[i, :, :width] for i in range(3)], ((1,), (1,))
            )

    rhs = rpart[tuple(bits)] - RIDGE * weight_ref[...]
    for j in range(count):
        here = block(j)
        y = rhs[:, here]
        if j:
            y = y - dot32(ys[:, : B * j], pieces(w_ref[here, : B * j]), ((1,), (1,)))
        ys[:, here] = stacked(y)

    def gather(c):
        def start(s):
            mine = index(c, s, bits[ORDERS[c][s]])
            return send(
                out_ref.at[mine], out_ref.at[mine], ag_s.at[c, s], ag_r.at[c, s], partners[ORDERS[c][s]]
            )

        copy = start(STAGES - 1)
        for s in range(STAGES - 1, -1, -1):
            yield
            copy.wait()
            if s:
                copy = start(s - 1)

    gathers = []
    for j in range(count - 1, -1, -1):
        here = block(j)
        x = dot32(ys[:, here], pieces(w_ref[here, here]), ((1,), (0,)))
        if j < count - 1:
            after = slice(B * j + B, n)
            x = x - dot32(ys[:, after], pieces(w_ref[after, here]), ((1,), (0,)))
        out_ref[tuple(bits) + (slice(None), here)] = x
        ys[:, here] = stacked(x)
        if B * j % lanes == 0:
            for held in gathers:
                next(held, None)
            gathers.append(gather(B * j // lanes))
            next(gathers[-1])
    for _ in range(STAGES):
        for held in gathers:
            next(held, None)


HOOKS = (
    ("start", "ABC" + "AABAABCAABABCAABACABA"),
    ((0, 0), "BC"),
    ((0, 1), "BC"),
    ((0, 2), "BCBCBBB"),
    ((1, 0), "C"),
    ((1, 1), "C"),
    ((2, 0), "C"),
    ((2, 1), "C"),
    ((3, 0), "CC"),
    ((3, 2), "CCCCCR"),
    ((5, 0), "R"),
    ((6, 0), "R"),
    ((7, 0), "R"),
    ((8, 0), "R"),
    ((9, 0), "R"),
    ((10, 0), "RR"),
)


def sweep_over_all_rows(phi, own, labels, own_weights, padded):
    rows, n = phi.shape
    classes = own.shape[1]
    total = packed_rows(n)
    per = padded >> STAGES
    blocks = (2,) * STAGES + (per, n)
    vmem = pl.BlockSpec(memory_space=pltpu.VMEM)
    sem = pltpu.SemaphoreType.DMA
    f32, bf16 = jnp.float32, jnp.bfloat16
    solution, residual = pl.pallas_call(
        sweep_kernel,
        out_shape=(
            jax.ShapeDtypeStruct(blocks, f32),
            jax.ShapeDtypeStruct((rows, classes), f32),
        ),
        in_specs=[vmem] * 4,
        out_specs=(vmem, vmem),
        scratch_shapes=[
            pltpu.VMEM((n, rows), bf16),
            pltpu.VMEM((total, B), f32),
            pltpu.VMEM((total, B), f32),
            pltpu.VMEM((total, B), f32),
            pltpu.VMEM(blocks, f32),
            pltpu.VMEM(blocks, f32),
            pltpu.VMEM((rows, classes), f32),
            pltpu.VMEM((rows, padded), bf16),
            pltpu.VMEM((padded, rows), bf16),
            pltpu.VMEM((n, n), f32),
            pltpu.VMEM((3, B, n), bf16),
            pltpu.VMEM((3, B, B), bf16),
            pltpu.VMEM((3 * per, n), bf16),
            pltpu.VMEM((B, B), f32),
            pltpu.VMEM((48, B), bf16),
            pltpu.VMEM((48, B), bf16),
            pltpu.VMEM((8, B), f32),
            pltpu.VMEM((72, B), f32),
            sem((2,)),
            *[sem((3, COLORS, STAGES))] * 4,
            *[sem((COLORS, STAGES))] * 4,
        ],
        compiler_params=pltpu.CompilerParams(
            vmem_limit_bytes=VMEM_LIMIT, collective_id=0, has_side_effects=True
        ),
        cost_estimate=pl.CostEstimate(
            flops=2 * n * n * n, bytes_accessed=300_000_000, transcendentals=0
        ),
        name="sweep_over_all_rows",
    )(phi, own, labels.reshape(rows, 1), own_weights)
    return solution.reshape(padded, n), residual


def body(inputs, labels, frequencies, phases, weights):
    groups = lax.axis_size("grp")
    width = frequencies.shape[1]
    classes = weights.shape[1]
    padded = -(-classes // 1024) * 1024
    scale = (2.0 / (groups * width)) ** 0.5
    swap = [(0, 1), (1, 0)]
    arg = (
        jnp.dot(inputs.astype(jnp.float32), frequencies, precision=lax.Precision.HIGHEST)
        + phases[None, :]
    )
    phi = (scale * jnp.cos(arg)).astype(jnp.bfloat16)
    own = jnp.dot(phi, weights.astype(jnp.bfloat16), preferred_element_type=jnp.float32)
    bits, _ = place()
    piece = 0
    for bit in bits:
        piece = piece * 2 + bit
    per = padded // 64
    start = jnp.minimum(piece * per, classes - per)
    beyond = piece * per - start
    kept = lax.dynamic_slice(weights, (0, start), (width, per)).T
    own_weights = jnp.zeros_like(kept)
    for shift in sorted({max(0, p * per - (classes - per)) for p in range(64)}):
        if shift < per:
            moved = jnp.pad(kept[shift:, :], ((0, shift), (0, 0)))
            own_weights = jnp.where(beyond == shift, moved, own_weights)

    solution, residual = sweep_over_all_rows(phi, own, labels, own_weights, padded)
    solution = solution[:classes]
    step = DAMP * solution
    delta = lax.dot_general(
        phi, step.astype(jnp.bfloat16), (((1,), (1,)), ((), ())), preferred_element_type=jnp.float32
    )
    change = delta + lax.ppermute(delta, "grp", swap)
    return (weights + step.T, residual - change)


def solution(mesh):
    return jax.shard_map(
        body,
        mesh=mesh,
        in_specs=(P("row", None), P("row"), P(None, "grp"), P("grp"), P("grp", None)),
        out_specs=(P("grp", None), P("row", None)),
        check_vma=False,
    )
```

```python
import functools

import jax
import jax.numpy as jnp
from jax import lax
from jax.experimental import pallas as pl
from jax.experimental.pallas import tpu as pltpu
from jax.sharding import PartitionSpec as P

RIDGE = 1.0
DAMP = 0.5
MESH = pl.DeviceIdType.MESH
B = 128
VMEM_LIMIT = 62 * 1024 * 1024

CORE, XA, XB, YA, YB, ZH = range(6)
ORDERS = (
    (CORE, XA, XB, YA, YB, ZH),
    (CORE, YA, YB, XA, XB, ZH),
    (CORE, XB, XA, YB, YA, ZH),
    (CORE, YB, YA, XB, XA, ZH),
)
COLORS = len(ORDERS)
STAGES = 6


def place():
    r = lax.axis_index("row")
    core, y, x, z = lax.rem(r, 2), lax.rem(r // 2, 4), lax.rem(r // 8, 4), r // 32
    at = lambda z, x, y, core: ((z * 4 + x) * 4 + y) * 2 + core
    flip = lambda q: q + 1 - 2 * lax.rem(q, 2)
    bits = (core, lax.rem((x + 1) // 2, 2), x // 2, lax.rem((y + 1) // 2, 2), y // 2, z)
    partners = (
        at(z, x, y, 1 - core),
        at(z, flip(x), y, core),
        at(z, 3 - x, y, core),
        at(z, x, flip(y), core),
        at(z, x, 3 - y, core),
        at(1 - z, x, y, core),
    )
    return bits, partners


def send(src, dst, send_sem, recv_sem, partner):
    copy = pltpu.make_async_remote_copy(
        src_ref=src,
        dst_ref=dst,
        send_sem=send_sem,
        recv_sem=recv_sem,
        device_id={"row": partner},
        device_id_type=MESH,
    )
    copy.start()
    return copy


def packed_offsets(n):
    return [sum(n - B * i for i in range(j)) for j in range(n // B + 1)]


def packed_rows(n):
    return -(-packed_offsets(n)[-1] // 2048) * 2048


def pieces(v):
    high = v.astype(jnp.bfloat16)
    rest = v - high.astype(jnp.float32)
    middle = rest.astype(jnp.bfloat16)
    return high, middle, (rest - middle.astype(jnp.float32)).astype(jnp.bfloat16)


def dot32(stack, right, dims):
    m = stack.shape[0] // 3
    dot = functools.partial(
        lax.dot_general, dimension_numbers=(dims, ((), ())), preferred_element_type=jnp.float32
    )
    high, middle, low = dot(stack, right[0]), dot(stack[: 2 * m], right[1]), dot(stack[:m], right[2])
    return high[:m] + ((high[m : 2 * m] + middle[:m]) + (high[2 * m :] + middle[m:] + low))


def stacked(v):
    return jnp.concatenate(pieces(v), axis=0)


def tree(t):
    return ((t[0] + t[1]) + (t[2] + t[3])) + ((t[4] + t[5]) + (t[6] + t[7]))


def key(i, j):
    return (i, j) if i >= j else (j, i)


def inverse8(a):
    for p in range(0, 8, 2):
        q = p + 1
        first, cross, second = a[p, p], a[q, p], a[q, q]
        det = first * second - cross * cross
        r = pl.reciprocal(det, approx=True)
        r = r * (2.0 - det * r)
        r = r * (2.0 - det * r)
        e, f, h = second * r, -(cross * r), first * r
        others = [i for i in range(8) if i not in (p, q)]
        u = {i: a[key(i, p)] for i in others}
        v = {i: a[key(i, q)] for i in others}
        mu = {i: u[i] * e + v[i] * f for i in others}
        mv = {i: u[i] * f + v[i] * h for i in others}
        for i in others:
            for j in others:
                if j <= i:
                    a[i, j] = a[i, j] - (mu[i] * u[j] + mv[i] * v[j])
        for i in others:
            a[key(i, p)], a[key(i, q)] = mu[i], mv[i]
        a[p, p], a[q, p], a[q, q] = -e, -f, -h
    return a


def inverse(block, scratch, parts):
    d_ref, p_ref, q_ref, t_ref, s_ref = scratch
    tile = (8, B)
    lane = lax.broadcasted_iota(jnp.int32, tile, 1)
    sub = lax.broadcasted_iota(jnp.int32, tile, 0)
    lanes = lax.broadcasted_iota(jnp.int32, (B, B), 1)
    d_ref[...] = block
    p_ref[...] = jnp.zeros(p_ref.shape, p_ref.dtype)
    q_ref[...] = jnp.zeros(q_ref.shape, q_ref.dtype)
    t_ref[...] = jnp.zeros(tile, jnp.float32)

    def columns(v, k):
        return [
            jnp.take_along_axis(v, jnp.full(tile, k + q, jnp.int32), axis=1) for q in range(8)
        ]

    def late():
        return lax.dot_general(
            p_ref[...], q_ref[...], (((0,), (0,)), ((), ())), preferred_element_type=jnp.float32
        )

    def step(b, top, also):
        k = pl.multiple_of(b * 8, 8)
        was = pl.multiple_of(lax.rem(k + B - 8, B), 8)
        update = late()
        below = d_ref[pl.ds(pl.multiple_of(lax.rem(k + 8, B), 8), 8), :]
        before = jnp.logical_and(jnp.logical_and(lane >= was, lane < was + 8), k > 0)
        cols = columns(below, was)
        below = jnp.where(before, 0.0, below) + tree(
            [cols[p] * jnp.broadcast_to(t_ref[p : p + 1, :], tile) for p in range(8)]
        )
        for q, col in enumerate(columns(top, k)):
            s_ref[8 * q : 8 * q + 8, :] = col
        a = {}
        for q in range(8):
            for p in range(q, 8):
                a[p, q] = jnp.broadcast_to(s_ref[8 * q + p : 8 * q + p + 1, :], tile)
        a = inverse8(a)
        now = jnp.logical_and(lane >= k, lane < k + 8)
        s_ref[64:72, :] = jnp.where(now, jnp.where(lane - k == sub, -1.0, 0.0), top)
        rows = [jnp.broadcast_to(s_ref[64 + q : 65 + q, :], tile) for q in range(8)]
        swept = [tree([a[key(p, q)] * rows[q] for q in range(8)]) for p in range(8)]
        cols = columns(below, k)
        below = jnp.where(now, 0.0, below) + tree([cols[p] * swept[p] for p in range(8)])
        strip = swept[0]
        for p in range(1, 8):
            strip = jnp.where(sub == p, swept[p], strip)
        place = lanes - was
        done = jnp.logical_and(k > 0, jnp.logical_and(place >= 0, place < 8))
        d_ref[...] = jnp.where(done, 0.0, d_ref[...]) + update
        d_ref[pl.ds(was, 8), :] = jnp.where(k > 0, -t_ref[...], d_ref[pl.ds(was, 8), :])
        uh, um, ul = (v.astype(jnp.float32) for v in pieces(top))
        th, tm, tl = (v.astype(jnp.float32) for v in pieces(strip))
        p_ref[...] = jnp.concatenate([uh, uh, um, uh, um, ul], axis=0).astype(jnp.bfloat16)
        q_ref[...] = jnp.concatenate([th, tm, th, tl, tm, th], axis=0).astype(jnp.bfloat16)
        t_ref[...] = strip
        if also is not None:
            also(b)
        return below

    top = block[:8, :]
    begin = 0
    for steps, also, after in parts:
        if steps:
            top = lax.fori_loop(
                begin, begin + steps, lambda b, v, also=also: step(b, v, also), top
            )
        begin += steps
        after()
    d = jnp.where(lanes >= B - 8, 0.0, d_ref[...]) + late()
    return -jnp.concatenate([d[: B - 8, :], -t_ref[...]], axis=0)


def sweep_kernel(
    phi_ref, all_ref, label_ref,
    out_ref, res_ref, delta_ref,
    phit, gpart, gland, a_ref, rpart, rland, held_ref, own_ref, other, early, late_ref, low_ref, lowt, w_ref, rs, dv, ys,
    d_ref, p_ref, q_ref, t_ref, s_ref,
    swap_sem, copy_sem, grs_s, grs_r, gag_s, gag_r, rs_s, rs_r, ag_s, ag_r,
):
    bits, partners = place()
    group = lax.axis_index("grp")
    n = phi_ref.shape[1]
    count = n // B
    offsets = packed_offsets(n)
    total = a_ref.shape[0]
    classes = all_ref.shape[0]
    per = out_ref.shape[-2]
    half = lowt.shape[0] // 2
    lanes = n // COLORS
    block = lambda j: slice(B * j, B * j + B)

    bring = pltpu.make_async_copy(all_ref, held_ref.at[pl.ds(0, classes), :], copy_sem)
    bring.start()
    held_ref[classes:, :] = jnp.zeros((held_ref.shape[0] - classes, n), jnp.float32)
    for j in range(count):
        phit[block(j), :] = phi_ref[:, block(j)].T
    for j in range(count):
        gpart[offsets[j] : offsets[j + 1], :] = lax.dot_general(
            phit[B * j :, :],
            phit[block(j), :],
            (((1,), (1,)), ((), ())),
            preferred_element_type=jnp.float32,
        )
    gpart[offsets[-1] :, :] = jnp.zeros((total - offsets[-1], B), jnp.float32)

    barrier = pltpu.get_barrier_semaphore()
    pl.semaphore_signal(barrier, inc=1, device_id={"grp": 1 - group}, device_id_type=MESH)
    for partner in partners:
        pl.semaphore_signal(barrier, inc=1, device_id={"row": partner}, device_id_type=MESH)
    pl.semaphore_wait(barrier, len(partners) + 1)

    swap = pltpu.make_async_remote_copy(
        src_ref=own_ref,
        dst_ref=other,
        send_sem=swap_sem.at[0],
        recv_sem=swap_sem.at[1],
        device_id={"grp": 1 - group},
        device_id_type=MESH,
    )

    def own_prediction():
        bring.wait()
        for at in range(0, classes, B):
            cols = slice(at, min(at + B, classes))
            own_ref[:, cols] = lax.dot_general(
                phi_ref[...],
                held_ref[cols, :].astype(jnp.bfloat16),
                (((1,), (1,)), ((), ())),
                preferred_element_type=jnp.float32,
            )
        swap.start()
        yield

    def gram_wave(w, base, rows):
        span = rows // COLORS
        low = [jnp.int32(base + span * c) for c in range(COLORS)]

        def reduce_start(c, s, src):
            size = span >> (s + 1)
            axis = ORDERS[c][s]
            give = pl.multiple_of(low[c] + (1 - bits[axis]) * size, 8)
            low[c] = low[c] + bits[axis] * size
            land = base + span * c + (span - (span >> s))
            return send(
                src.at[pl.ds(give, size), :],
                gland.at[pl.ds(land, size), :],
                grs_s.at[w, c, s],
                grs_r.at[w, c, s],
                partners[axis],
            )

        def gather_start(c, s):
            size = span >> (s + 1)
            axis = ORDERS[c][s]
            mine = pl.ds(pl.multiple_of(low[c], 8), size)
            low[c] = low[c] - bits[axis] * size
            return send(
                a_ref.at[mine, :], a_ref.at[mine, :], gag_s.at[w, c, s], gag_r.at[w, c, s], partners[axis]
            )

        pending = [reduce_start(c, 0, gpart) for c in range(COLORS)]
        yield
        for s in range(STAGES):
            size = span >> (s + 1)
            to = a_ref if s == STAGES - 1 else gpart
            step = min(size, 256)
            for c in range(COLORS):
                pending[c].wait()
                land = base + span * c + (span - (span >> s))
                here = low[c]

                @pl.loop(0, size // step)
                def _(i):
                    q = pl.ds(pl.multiple_of(here + i * step, 8), step)
                    to[q, :] = gpart[q, :] + gland[pl.ds(pl.multiple_of(land + i * step, 8), step), :]

                pending[c] = reduce_start(c, s + 1, gpart) if s < STAGES - 1 else gather_start(c, s)
            yield
        for s in range(STAGES - 1, -1, -1):
            for c in range(COLORS):
                pending[c].wait()
                if s:
                    pending[c] = gather_start(c, s - 1)
            yield

    def index(c, s, value, h=slice(None)):
        where = [slice(None)] * STAGES
        for axis in ORDERS[c][:s]:
            where[axis] = bits[axis]
        where[ORDERS[c][s]] = value
        return (h,) + tuple(where) + (slice(None), pl.ds(lanes * c, lanes))

    def rhs_sum():
        swap.wait()
        low_ref[...] = jnp.zeros(low_ref.shape, low_ref.dtype)
        for i in range(phi_ref.shape[0] // B):
            label = jnp.broadcast_to(label_ref[:, block(i)], (B, B)).T
            for at in range(0, classes, B):
                cols = slice(at, min(at + B, classes))
                wide = cols.stop - cols.start
                hot = label[:, :wide] == at + lax.broadcasted_iota(jnp.int32, (B, wide), 1)
                residual = hot.astype(jnp.float32) - (own_ref[block(i), cols] + other[block(i), cols])
                res_ref[block(i), cols] = residual
                low_ref[block(i), cols] = residual.astype(jnp.bfloat16)
        for i in range(lowt.shape[0] // B):
            lowt[block(i), :] = low_ref[:, block(i)].T
        for i in range(8):
            rpart[i // 4, i // 2 % 2, i % 2] = lax.dot_general(
                lowt[i * 16 * per : (i + 1) * 16 * per, :],
                phi_ref[...],
                (((1,), (0,)), ((), ())),
                preferred_element_type=jnp.float32,
            ).reshape(2, 2, 2, 2, per, n)

        def start(c, s):
            axis = ORDERS[c][s]
            return send(
                rpart.at[index(c, s, 1 - bits[axis])],
                rland.at[index(c, s, bits[axis])],
                rs_s.at[c, s],
                rs_r.at[c, s],
                partners[axis],
            )

        pending = [start(c, 0) for c in range(COLORS)]
        yield
        for s in range(STAGES):
            for c in range(COLORS):
                pending[c].wait()
                mine = index(c, s, bits[ORDERS[c][s]])
                rpart[mine] = rpart[mine] + rland[index(c, s, 1 - bits[ORDERS[c][s]])]
                if s < STAGES - 1:
                    pending[c] = start(c, s + 1)
            yield

    waves = dict(
        A=gram_wave(0, 0, 2048),
        B=gram_wave(1, 2048, 4096),
        C=gram_wave(2, 6144, total - 6144),
        O=own_prediction(),
        R=rhs_sum(),
    )

    def go(names):
        for name in names:
            next(waves[name], None)

    hooks = dict(HOOKS)

    scratch = (d_ref, p_ref, q_ref, t_ref, s_ref)
    eye = (
        lax.broadcasted_iota(jnp.int32, (B, B), 0) == lax.broadcasted_iota(jnp.int32, (B, B), 1)
    ).astype(jnp.float32)
    go(hooks["start"])
    system = a_ref[:B, :] + RIDGE * eye
    for j in range(count):
        go(hooks.get((j, 0), ""))
        here = block(j)
        width = B * j

        def row_of(t, j=j, here=here, width=width):
            at = pl.ds(pl.multiple_of(t * B, B), B)
            old = pl.ds(pl.multiple_of(offsets[j - 1] + (t - j + 1) * B, B), B)
            new = pl.ds(pl.multiple_of(offsets[j] + (t - j) * B, B), B)
            w_ref[at, block(j - 1)] = dot32(
                stacked(a_ref[old, :]), (dv[0], dv[1], dv[2]), ((1,), (0,))
            )
            a_ref[new, :] = a_ref[new, :] - dot32(
                stacked(w_ref[at, :width]), [rs[i, :, :width] for i in range(3)], ((1,), (1,))
            )

        with_rows = count - 1 - j if j else 0
        parts = [
            (with_rows, lambda b, j=j, f=row_of: f(j + 1 + b), lambda j=j: go(hooks.get((j, 1), ""))),
            (B // 8 - with_rows, None, lambda j=j: go(hooks.get((j, 2), ""))),
        ]
        inv = inverse(system, scratch, parts)
        w_ref[here, here] = inv
        if j < count - 1:
            dv[0], dv[1], dv[2] = pieces(inv)
            after = block(j + 1)
            w_ref[after, here] = dot32(
                stacked(a_ref[offsets[j] + B : offsets[j] + 2 * B, :]),
                (dv[0], dv[1], dv[2]),
                ((1,), (0,)),
            )
            for k in range(j + 1):
                at = offsets[k] + (j + 1 - k) * B
                rs[0, :, block(k)], rs[1, :, block(k)], rs[2, :, block(k)] = pieces(
                    a_ref[at : at + B, :]
                )
            width = B * (j + 1)
            system = (a_ref[offsets[j + 1] : offsets[j + 1] + B, :] + RIDGE * eye) - dot32(
                stacked(w_ref[after, :width]), [rs[i, :, :width] for i in range(3)], ((1,), (1,))
            )

    mine = (slice(None),) + tuple(bits)
    piece = 0
    for bit in bits:
        piece = piece * 2 + bit
    weights = [
        held_ref[pl.ds(pl.multiple_of(h * half + piece * per, per), per), :] for h in range(2)
    ]
    rhs = rpart[mine].reshape(2 * per, n) - RIDGE * jnp.concatenate(weights, axis=0)
    for j in range(count):
        here = block(j)
        y = rhs[:, here]
        if j:
            y = y - dot32(ys[:, : B * j], pieces(w_ref[here, : B * j]), ((1,), (1,)))
        ys[:, here] = stacked(y)

    def gather(c, h):
        def start(s):
            at = index(c, s, bits[ORDERS[c][s]], h)
            return send(
                out_ref.at[at],
                out_ref.at[at],
                ag_s.at[h, c, s],
                ag_r.at[h, c, s],
                partners[ORDERS[c][s]],
            )

        copy = start(STAGES - 1)
        for s in range(STAGES - 1, -1, -1):
            yield
            copy.wait()
            if s:
                copy = start(s - 1)

    gathers = ([], [])
    for j in range(count - 1, -1, -1):
        here = block(j)
        x = dot32(ys[:, here], pieces(w_ref[here, here]), ((1,), (0,)))
        if j < count - 1:
            after = slice(B * j + B, n)
            x = x - dot32(ys[:, after], pieces(w_ref[after, here]), ((1,), (0,)))
        out_ref[mine + (slice(None), here)] = x.reshape(2, per, B)
        ys[:, here] = stacked(x)
        if B * j % lanes == 0:
            for held in gathers[0]:
                next(held, None)
            gathers[0].append(gather(B * j // lanes, 0))
            next(gathers[0][-1])
    for r in range(STAGES):
        for held in gathers[0]:
            next(held, None)
        if r == 0:
            gathers[1].extend(gather(c, 1) for c in range(COLORS - 1, -1, -1))
        for held in gathers[1]:
            next(held, None)
    def predictions(h, i):
        return lax.dot_general(
            phi_ref[...],
            (DAMP * out_ref[h, i // 2, i % 2].reshape(16 * per, n)).astype(jnp.bfloat16),
            (((1,), (1,)), ((), ())),
            preferred_element_type=jnp.float32,
        )

    for i in range(4):
        early[:, i * 16 * per : (i + 1) * 16 * per] = predictions(0, i)
    change = pltpu.make_async_remote_copy(
        src_ref=early,
        dst_ref=late_ref,
        send_sem=swap_sem.at[2],
        recv_sem=swap_sem.at[3],
        device_id={"grp": 1 - group},
        device_id_type=MESH,
    )
    change.start()
    for held in gathers[1]:
        next(held, None)
    for i in range(4):
        at = i * 16 * per
        wide = min(16 * per, classes - half - at)
        delta_ref[:, at : at + wide] = predictions(1, i)[:, :wide]
    change.wait()
    res_ref[:, :half] = res_ref[:, :half] - (early[...] + late_ref[...])


HOOKS = (
    ("start", "ABCO" + "ABC" * 12),
    ((0, 0), "R"),
    ((2, 0), "R"),
    ((4, 0), "R"),
    ((6, 0), "R"),
    ((7, 0), "R"),
    ((8, 0), "R"),
    ((9, 0), "R"),
)


def sweep_over_all_rows(phi, weights, labels, padded):
    rows, n = phi.shape
    classes = weights.shape[0]
    total = packed_rows(n)
    per = padded >> (STAGES + 1)
    blocks = (2,) * (STAGES + 1) + (per, n)
    vmem = pl.BlockSpec(memory_space=pltpu.VMEM)
    sem = pltpu.SemaphoreType.DMA
    f32, bf16 = jnp.float32, jnp.bfloat16
    solution, residual, delta = pl.pallas_call(
        sweep_kernel,
        out_shape=(
            jax.ShapeDtypeStruct(blocks, f32),
            jax.ShapeDtypeStruct((rows, classes), f32),
            jax.ShapeDtypeStruct((rows, classes - padded // 2), f32),
        ),
        in_specs=[vmem, pl.BlockSpec(memory_space=pl.ANY), vmem],
        out_specs=(vmem, vmem, vmem),
        scratch_shapes=[
            pltpu.VMEM((n, rows), bf16),
            pltpu.VMEM((total, B), f32),
            pltpu.VMEM((total, B), f32),
            pltpu.VMEM((total, B), f32),
            pltpu.VMEM(blocks, f32),
            pltpu.VMEM(blocks, f32),
            pltpu.VMEM((padded, n), f32),
            pltpu.VMEM((rows, classes), f32),
            pltpu.VMEM((rows, classes), f32),
            pltpu.VMEM((rows, padded // 2), f32),
            pltpu.VMEM((rows, padded // 2), f32),
            pltpu.VMEM((rows, padded), bf16),
            pltpu.VMEM((padded, rows), bf16),
            pltpu.VMEM((n, n), f32),
            pltpu.VMEM((3, B, n), bf16),
            pltpu.VMEM((3, B, B), bf16),
            pltpu.VMEM((6 * per, n), bf16),
            pltpu.VMEM((B, B), f32),
            pltpu.VMEM((48, B), bf16),
            pltpu.VMEM((48, B), bf16),
            pltpu.VMEM((8, B), f32),
            pltpu.VMEM((72, B), f32),
            sem((4,)),
            sem,
            *[sem((3, COLORS, STAGES))] * 4,
            *[sem((COLORS, STAGES))] * 2,
            *[sem((2, COLORS, STAGES))] * 2,
        ],
        compiler_params=pltpu.CompilerParams(
            vmem_limit_bytes=VMEM_LIMIT, collective_id=0, has_side_effects=True
        ),
        cost_estimate=pl.CostEstimate(
            flops=2 * n * n * n, bytes_accessed=300_000_000, transcendentals=0
        ),
        name="sweep_over_all_rows",
    )(phi, weights, labels.reshape(1, rows))
    return solution.reshape(padded, n), residual, delta


def body(inputs, labels, frequencies, phases, weights):
    groups = lax.axis_size("grp")
    width = frequencies.shape[1]
    classes = weights.shape[1]
    padded = -(-classes // 1024) * 1024
    scale = (2.0 / (groups * width)) ** 0.5
    swap = [(0, 1), (1, 0)]
    arg = (
        jnp.dot(inputs.astype(jnp.float32), frequencies, precision=lax.Precision.HIGHEST)
        + phases[None, :]
    )
    phi = (scale * jnp.cos(arg)).astype(jnp.bfloat16)
    solution, residual, delta = sweep_over_all_rows(phi, weights.T, labels, padded)
    step = DAMP * solution[:classes]
    half = padded // 2
    change = delta + lax.ppermute(delta, "grp", swap)
    return (
        weights + step.T,
        jnp.concatenate([residual[:, :half], residual[:, half:] - change], axis=1),
    )


def solution(mesh):
    return jax.shard_map(
        body,
        mesh=mesh,
        in_specs=(P("row", None), P("row"), P(None, "grp"), P("grp"), P("grp", None)),
        out_specs=(P("grp", None), P("row", None)),
        check_vma=False,
    )
```

```python
import functools

import jax
import jax.numpy as jnp
from jax import lax
from jax.experimental import pallas as pl
from jax.experimental.pallas import tpu as pltpu
from jax.sharding import PartitionSpec as P

RIDGE = 1.0
DAMP = 0.5
MESH = pl.DeviceIdType.MESH
B = 128
VMEM_LIMIT = 62 * 1024 * 1024

CORE, XA, XB, YA, YB, ZH = range(6)
ORDERS = (
    (CORE, XA, XB, YA, YB, ZH),
    (CORE, YA, YB, XA, XB, ZH),
    (CORE, XB, XA, YB, YA, ZH),
    (CORE, YB, YA, XB, XA, ZH),
)
COLORS = len(ORDERS)
STAGES = 6


def place():
    r = lax.axis_index("row")
    core, y, x, z = lax.rem(r, 2), lax.rem(r // 2, 4), lax.rem(r // 8, 4), r // 32
    at = lambda z, x, y, core: ((z * 4 + x) * 4 + y) * 2 + core
    flip = lambda q: q + 1 - 2 * lax.rem(q, 2)
    bits = (core, lax.rem((x + 1) // 2, 2), x // 2, lax.rem((y + 1) // 2, 2), y // 2, z)
    partners = (
        at(z, x, y, 1 - core),
        at(z, flip(x), y, core),
        at(z, 3 - x, y, core),
        at(z, x, flip(y), core),
        at(z, x, 3 - y, core),
        at(1 - z, x, y, core),
    )
    return bits, partners


def send(src, dst, send_sem, recv_sem, partner):
    copy = pltpu.make_async_remote_copy(
        src_ref=src,
        dst_ref=dst,
        send_sem=send_sem,
        recv_sem=recv_sem,
        device_id={"row": partner},
        device_id_type=MESH,
    )
    copy.start()
    return copy


def packed_offsets(n):
    return [sum(n - B * i for i in range(j)) for j in range(n // B + 1)]


def packed_rows(n):
    return -(-packed_offsets(n)[-1] // 2048) * 2048


def pieces(v):
    high = v.astype(jnp.bfloat16)
    rest = v - high.astype(jnp.float32)
    middle = rest.astype(jnp.bfloat16)
    return high, middle, (rest - middle.astype(jnp.float32)).astype(jnp.bfloat16)


def dot32(stack, right, dims):
    m = stack.shape[0] // 3
    dot = functools.partial(
        lax.dot_general, dimension_numbers=(dims, ((), ())), preferred_element_type=jnp.float32
    )
    high, middle, low = dot(stack, right[0]), dot(stack[: 2 * m], right[1]), dot(stack[:m], right[2])
    return high[:m] + ((high[m : 2 * m] + middle[:m]) + (high[2 * m :] + middle[m:] + low))


def stacked(v):
    return jnp.concatenate(pieces(v), axis=0)


def tree(t):
    return ((t[0] + t[1]) + (t[2] + t[3])) + ((t[4] + t[5]) + (t[6] + t[7]))


def key(i, j):
    return (i, j) if i >= j else (j, i)


def inverse8(a):
    for p in range(0, 8, 2):
        q = p + 1
        first, cross, second = a[p, p], a[q, p], a[q, q]
        det = first * second - cross * cross
        r = pl.reciprocal(det, approx=True)
        r = r * (2.0 - det * r)
        r = r * (2.0 - det * r)
        e, f, h = second * r, -(cross * r), first * r
        others = [i for i in range(8) if i not in (p, q)]
        u = {i: a[key(i, p)] for i in others}
        v = {i: a[key(i, q)] for i in others}
        mu = {i: u[i] * e + v[i] * f for i in others}
        mv = {i: u[i] * f + v[i] * h for i in others}
        for i in others:
            for j in others:
                if j <= i:
                    a[i, j] = a[i, j] - (mu[i] * u[j] + mv[i] * v[j])
        for i in others:
            a[key(i, p)], a[key(i, q)] = mu[i], mv[i]
        a[p, p], a[q, p], a[q, q] = -e, -f, -h
    return a


def inverse(block, scratch, parts):
    d_ref, p_ref, q_ref, t_ref, s_ref = scratch
    tile = (8, B)
    lane = lax.broadcasted_iota(jnp.int32, tile, 1)
    sub = lax.broadcasted_iota(jnp.int32, tile, 0)
    lanes = lax.broadcasted_iota(jnp.int32, (B, B), 1)
    d_ref[...] = block
    p_ref[...] = jnp.zeros(p_ref.shape, p_ref.dtype)
    q_ref[...] = jnp.zeros(q_ref.shape, q_ref.dtype)
    t_ref[...] = jnp.zeros(tile, jnp.float32)

    def columns(v, k):
        return [
            jnp.take_along_axis(v, jnp.full(tile, k + q, jnp.int32), axis=1) for q in range(8)
        ]

    def late():
        return lax.dot_general(
            p_ref[...], q_ref[...], (((0,), (0,)), ((), ())), preferred_element_type=jnp.float32
        )

    def step(b, top, also):
        k = pl.multiple_of(b * 8, 8)
        was = pl.multiple_of(lax.rem(k + B - 8, B), 8)
        update = late()
        below = d_ref[pl.ds(pl.multiple_of(lax.rem(k + 8, B), 8), 8), :]
        before = jnp.logical_and(jnp.logical_and(lane >= was, lane < was + 8), k > 0)
        cols = columns(below, was)
        below = jnp.where(before, 0.0, below) + tree(
            [cols[p] * jnp.broadcast_to(t_ref[p : p + 1, :], tile) for p in range(8)]
        )
        for q, col in enumerate(columns(top, k)):
            s_ref[8 * q : 8 * q + 8, :] = col
        a = {}
        for q in range(8):
            for p in range(q, 8):
                a[p, q] = jnp.broadcast_to(s_ref[8 * q + p : 8 * q + p + 1, :], tile)
        a = inverse8(a)
        now = jnp.logical_and(lane >= k, lane < k + 8)
        s_ref[64:72, :] = jnp.where(now, jnp.where(lane - k == sub, -1.0, 0.0), top)
        rows = [jnp.broadcast_to(s_ref[64 + q : 65 + q, :], tile) for q in range(8)]
        swept = [tree([a[key(p, q)] * rows[q] for q in range(8)]) for p in range(8)]
        cols = columns(below, k)
        below = jnp.where(now, 0.0, below) + tree([cols[p] * swept[p] for p in range(8)])
        strip = swept[0]
        for p in range(1, 8):
            strip = jnp.where(sub == p, swept[p], strip)
        place = lanes - was
        done = jnp.logical_and(k > 0, jnp.logical_and(place >= 0, place < 8))
        d_ref[...] = jnp.where(done, 0.0, d_ref[...]) + update
        d_ref[pl.ds(was, 8), :] = jnp.where(k > 0, -t_ref[...], d_ref[pl.ds(was, 8), :])
        uh, um, ul = (v.astype(jnp.float32) for v in pieces(top))
        th, tm, tl = (v.astype(jnp.float32) for v in pieces(strip))
        p_ref[...] = jnp.concatenate([uh, uh, um, uh, um, ul], axis=0).astype(jnp.bfloat16)
        q_ref[...] = jnp.concatenate([th, tm, th, tl, tm, th], axis=0).astype(jnp.bfloat16)
        t_ref[...] = strip
        if also is not None:
            also(b)
        return below

    top = block[:8, :]
    begin = 0
    for steps, also, after in parts:
        if steps:
            top = lax.fori_loop(
                begin, begin + steps, lambda b, v, also=also: step(b, v, also), top
            )
        begin += steps
        after()
    d = jnp.where(lanes >= B - 8, 0.0, d_ref[...]) + late()
    return -jnp.concatenate([d[: B - 8, :], -t_ref[...]], axis=0)


def sweep_kernel(
    phi_ref, all_ref, label_ref,
    out_ref, res_ref, delta_ref,
    phit, gpart, gland, a_ref, rpart, rland, held_ref, own_ref, other, early, late_ref, low_ref, lowt, w_ref, rs, dv, ys,
    d_ref, p_ref, q_ref, t_ref, s_ref,
    swap_sem, copy_sem, grs_s, grs_r, gag_s, gag_r, rs_s, rs_r, ag_s, ag_r,
):
    bits, partners = place()
    group = lax.axis_index("grp")
    n = phi_ref.shape[1]
    count = n // B
    offsets = packed_offsets(n)
    total = a_ref.shape[0]
    classes = all_ref.shape[0]
    per = out_ref.shape[-2]
    half = lowt.shape[0] // 2
    lanes = n // COLORS
    block = lambda j: slice(B * j, B * j + B)

    bring = pltpu.make_async_copy(all_ref, held_ref.at[pl.ds(0, classes), :], copy_sem)
    bring.start()
    held_ref[classes:, :] = jnp.zeros((held_ref.shape[0] - classes, n), jnp.float32)
    barrier = pltpu.get_barrier_semaphore()
    pl.semaphore_signal(barrier, inc=1, device_id={"grp": 1 - group}, device_id_type=MESH)
    for partner in partners:
        pl.semaphore_signal(barrier, inc=1, device_id={"row": partner}, device_id_type=MESH)
    for j in range(count):
        phit[block(j), :] = phi_ref[:, block(j)].T

    def own_gram():
        gpart[offsets[-1] :, :] = jnp.zeros((total - offsets[-1], B), jnp.float32)
        for j in range(count):
            gpart[offsets[j] : offsets[j + 1], :] = lax.dot_general(
                phit[B * j :, :],
                phit[block(j), :],
                (((1,), (1,)), ((), ())),
                preferred_element_type=jnp.float32,
            )
            if offsets[j] < 2048 <= offsets[j + 1] or offsets[j] < 6144 <= offsets[j + 1]:
                yield

    swap = pltpu.make_async_remote_copy(
        src_ref=own_ref,
        dst_ref=other,
        send_sem=swap_sem.at[0],
        recv_sem=swap_sem.at[1],
        device_id={"grp": 1 - group},
        device_id_type=MESH,
    )

    def own_prediction():
        bring.wait()
        for at in range(0, classes, B):
            cols = slice(at, min(at + B, classes))
            own_ref[:, cols] = lax.dot_general(
                phi_ref[...],
                held_ref[cols, :].astype(jnp.bfloat16),
                (((1,), (1,)), ((), ())),
                preferred_element_type=jnp.float32,
            )
        swap.start()
        yield

    def gram_wave(w, base, rows):
        span = rows // COLORS
        low = [jnp.int32(base + span * c) for c in range(COLORS)]

        def reduce_start(c, s, src):
            size = span >> (s + 1)
            axis = ORDERS[c][s]
            give = pl.multiple_of(low[c] + (1 - bits[axis]) * size, 8)
            low[c] = low[c] + bits[axis] * size
            land = base + span * c + (span - (span >> s))
            return send(
                src.at[pl.ds(give, size), :],
                gland.at[pl.ds(land, size), :],
                grs_s.at[w, c, s],
                grs_r.at[w, c, s],
                partners[axis],
            )

        def gather_start(c, s):
            size = span >> (s + 1)
            axis = ORDERS[c][s]
            mine = pl.ds(pl.multiple_of(low[c], 8), size)
            low[c] = low[c] - bits[axis] * size
            return send(
                a_ref.at[mine, :], a_ref.at[mine, :], gag_s.at[w, c, s], gag_r.at[w, c, s], partners[axis]
            )

        pending = [reduce_start(c, 0, gpart) for c in range(COLORS)]
        yield
        for s in range(STAGES):
            size = span >> (s + 1)
            to = a_ref if s == STAGES - 1 else gpart
            step = min(size, 256)
            for c in range(COLORS):
                pending[c].wait()
                land = base + span * c + (span - (span >> s))
                here = low[c]

                @pl.loop(0, size // step)
                def _(i):
                    q = pl.ds(pl.multiple_of(here + i * step, 8), step)
                    to[q, :] = gpart[q, :] + gland[pl.ds(pl.multiple_of(land + i * step, 8), step), :]

                pending[c] = reduce_start(c, s + 1, gpart) if s < STAGES - 1 else gather_start(c, s)
            yield
        for s in range(STAGES - 1, -1, -1):
            for c in range(COLORS):
                pending[c].wait()
                if s:
                    pending[c] = gather_start(c, s - 1)
            yield

    def index(c, s, value, h=slice(None)):
        where = [slice(None)] * STAGES
        for axis in ORDERS[c][:s]:
            where[axis] = bits[axis]
        where[ORDERS[c][s]] = value
        return (h,) + tuple(where) + (slice(None), pl.ds(lanes * c, lanes))

    def rhs_sum():
        swap.wait()
        low_ref[...] = jnp.zeros(low_ref.shape, low_ref.dtype)
        for i in range(phi_ref.shape[0] // B):
            label = jnp.broadcast_to(label_ref[:, block(i)], (B, B)).T
            for at in range(0, classes, B):
                cols = slice(at, min(at + B, classes))
                wide = cols.stop - cols.start
                hot = label[:, :wide] == at + lax.broadcasted_iota(jnp.int32, (B, wide), 1)
                residual = hot.astype(jnp.float32) - (own_ref[block(i), cols] + other[block(i), cols])
                res_ref[block(i), cols] = residual
                low_ref[block(i), cols] = residual.astype(jnp.bfloat16)
        for i in range(lowt.shape[0] // B):
            lowt[block(i), :] = low_ref[:, block(i)].T
        for i in range(8):
            rpart[i // 4, i // 2 % 2, i % 2] = lax.dot_general(
                lowt[i * 16 * per : (i + 1) * 16 * per, :],
                phi_ref[...],
                (((1,), (0,)), ((), ())),
                preferred_element_type=jnp.float32,
            ).reshape(2, 2, 2, 2, per, n)

        def start(c, s):
            axis = ORDERS[c][s]
            return send(
                rpart.at[index(c, s, 1 - bits[axis])],
                rland.at[index(c, s, bits[axis])],
                rs_s.at[c, s],
                rs_r.at[c, s],
                partners[axis],
            )

        pending = [start(c, 0) for c in range(COLORS)]
        yield
        for s in range(STAGES):
            for c in range(COLORS):
                pending[c].wait()
                mine = index(c, s, bits[ORDERS[c][s]])
                rpart[mine] = rpart[mine] + rland[index(c, s, 1 - bits[ORDERS[c][s]])]
                if s < STAGES - 1:
                    pending[c] = start(c, s + 1)
            yield

    waves = dict(
        A=gram_wave(0, 0, 2048),
        B=gram_wave(1, 2048, 4096),
        C=gram_wave(2, 6144, total - 6144),
        O=own_prediction(),
        G=own_gram(),
        R=rhs_sum(),
    )

    def go(names):
        for name in names:
            next(waves[name], None)

    hooks = dict(HOOKS)

    scratch = (d_ref, p_ref, q_ref, t_ref, s_ref)
    eye = (
        lax.broadcasted_iota(jnp.int32, (B, B), 0) == lax.broadcasted_iota(jnp.int32, (B, B), 1)
    ).astype(jnp.float32)
    go("G")
    pl.semaphore_wait(barrier, len(partners) + 1)
    go(hooks["start"])
    system = a_ref[:B, :] + RIDGE * eye
    for j in range(count):
        go(hooks.get((j, 0), ""))
        here = block(j)
        width = B * j

        def row_of(t, j=j, here=here, width=width):
            at = pl.ds(pl.multiple_of(t * B, B), B)
            old = pl.ds(pl.multiple_of(offsets[j - 1] + (t - j + 1) * B, B), B)
            new = pl.ds(pl.multiple_of(offsets[j] + (t - j) * B, B), B)
            w_ref[at, block(j - 1)] = dot32(
                stacked(a_ref[old, :]), (dv[0], dv[1], dv[2]), ((1,), (0,))
            )
            a_ref[new, :] = a_ref[new, :] - dot32(
                stacked(w_ref[at, :width]), [rs[i, :, :width] for i in range(3)], ((1,), (1,))
            )

        with_rows = count - 1 - j if j else 0
        parts = [
            (with_rows, lambda b, j=j, f=row_of: f(j + 1 + b), lambda j=j: go(hooks.get((j, 1), ""))),
            (B // 8 - with_rows, None, lambda j=j: go(hooks.get((j, 2), ""))),
        ]
        inv = inverse(system, scratch, parts)
        w_ref[here, here] = inv
        if j < count - 1:
            dv[0], dv[1], dv[2] = pieces(inv)
            after = block(j + 1)
            w_ref[after, here] = dot32(
                stacked(a_ref[offsets[j] + B : offsets[j] + 2 * B, :]),
                (dv[0], dv[1], dv[2]),
                ((1,), (0,)),
            )
            for k in range(j + 1):
                at = offsets[k] + (j + 1 - k) * B
                rs[0, :, block(k)], rs[1, :, block(k)], rs[2, :, block(k)] = pieces(
                    a_ref[at : at + B, :]
                )
            width = B * (j + 1)
            system = (a_ref[offsets[j + 1] : offsets[j + 1] + B, :] + RIDGE * eye) - dot32(
                stacked(w_ref[after, :width]), [rs[i, :, :width] for i in range(3)], ((1,), (1,))
            )

    mine = (slice(None),) + tuple(bits)
    piece = 0
    for bit in bits:
        piece = piece * 2 + bit
    weights = [
        held_ref[pl.ds(pl.multiple_of(h * half + piece * per, per), per), :] for h in range(2)
    ]
    rhs = rpart[mine].reshape(2 * per, n) - RIDGE * jnp.concatenate(weights, axis=0)
    for j in range(count):
        here = block(j)
        y = rhs[:, here]
        if j:
            y = y - dot32(ys[:, : B * j], pieces(w_ref[here, : B * j]), ((1,), (1,)))
        ys[:, here] = stacked(y)

    def gather(c, h):
        def start(s):
            at = index(c, s, bits[ORDERS[c][s]], h)
            return send(
                out_ref.at[at],
                out_ref.at[at],
                ag_s.at[h, c, s],
                ag_r.at[h, c, s],
                partners[ORDERS[c][s]],
            )

        copy = start(STAGES - 1)
        for s in range(STAGES - 1, -1, -1):
            yield
            copy.wait()
            if s:
                copy = start(s - 1)

    gathers = ([], [])
    for j in range(count - 1, -1, -1):
        here = block(j)
        x = dot32(ys[:, here], pieces(w_ref[here, here]), ((1,), (0,)))
        if j < count - 1:
            after = slice(B * j + B, n)
            x = x - dot32(ys[:, after], pieces(w_ref[after, here]), ((1,), (0,)))
        out_ref[mine + (slice(None), here)] = x.reshape(2, per, B)
        ys[:, here] = stacked(x)
        if B * j % lanes == 0:
            for held in gathers[0]:
                next(held, None)
            gathers[0].append(gather(B * j // lanes, 0))
            next(gathers[0][-1])
    for r in range(STAGES):
        for held in gathers[0]:
            next(held, None)
        if r == 0:
            gathers[1].extend(gather(c, 1) for c in range(COLORS - 1, -1, -1))
        for held in gathers[1]:
            next(held, None)
    def predictions(h, i):
        return lax.dot_general(
            phi_ref[...],
            (DAMP * out_ref[h, i // 2, i % 2].reshape(16 * per, n)).astype(jnp.bfloat16),
            (((1,), (1,)), ((), ())),
            preferred_element_type=jnp.float32,
        )

    for i in range(4):
        early[:, i * 16 * per : (i + 1) * 16 * per] = predictions(0, i)
    change = pltpu.make_async_remote_copy(
        src_ref=early,
        dst_ref=late_ref,
        send_sem=swap_sem.at[2],
        recv_sem=swap_sem.at[3],
        device_id={"grp": 1 - group},
        device_id_type=MESH,
    )
    change.start()
    for held in gathers[1]:
        next(held, None)
    for i in range(4):
        at = i * 16 * per
        wide = min(16 * per, classes - half - at)
        delta_ref[:, at : at + wide] = predictions(1, i)[:, :wide]
    change.wait()
    res_ref[:, :half] = res_ref[:, :half] - (early[...] + late_ref[...])


HOOKS = (
    ("start", "AGBGCO" + "ABC" * 12),
    ((0, 0), "R"),
    ((2, 0), "R"),
    ((4, 0), "R"),
    ((6, 0), "R"),
    ((7, 0), "R"),
    ((8, 0), "R"),
    ((9, 0), "R"),
)


def sweep_over_all_rows(phi, weights, labels, padded):
    rows, n = phi.shape
    classes = weights.shape[0]
    total = packed_rows(n)
    per = padded >> (STAGES + 1)
    blocks = (2,) * (STAGES + 1) + (per, n)
    vmem = pl.BlockSpec(memory_space=pltpu.VMEM)
    sem = pltpu.SemaphoreType.DMA
    f32, bf16 = jnp.float32, jnp.bfloat16
    solution, residual, delta = pl.pallas_call(
        sweep_kernel,
        out_shape=(
            jax.ShapeDtypeStruct(blocks, f32),
            jax.ShapeDtypeStruct((rows, classes), f32),
            jax.ShapeDtypeStruct((rows, classes - padded // 2), f32),
        ),
        in_specs=[vmem, pl.BlockSpec(memory_space=pl.ANY), vmem],
        out_specs=(vmem, vmem, vmem),
        scratch_shapes=[
            pltpu.VMEM((n, rows), bf16),
            pltpu.VMEM((total, B), f32),
            pltpu.VMEM((total, B), f32),
            pltpu.VMEM((total, B), f32),
            pltpu.VMEM(blocks, f32),
            pltpu.VMEM(blocks, f32),
            pltpu.VMEM((padded, n), f32),
            pltpu.VMEM((rows, classes), f32),
            pltpu.VMEM((rows, classes), f32),
            pltpu.VMEM((rows, padded // 2), f32),
            pltpu.VMEM((rows, padded // 2), f32),
            pltpu.VMEM((rows, padded), bf16),
            pltpu.VMEM((padded, rows), bf16),
            pltpu.VMEM((n, n), f32),
            pltpu.VMEM((3, B, n), bf16),
            pltpu.VMEM((3, B, B), bf16),
            pltpu.VMEM((6 * per, n), bf16),
            pltpu.VMEM((B, B), f32),
            pltpu.VMEM((48, B), bf16),
            pltpu.VMEM((48, B), bf16),
            pltpu.VMEM((8, B), f32),
            pltpu.VMEM((72, B), f32),
            sem((4,)),
            sem,
            *[sem((3, COLORS, STAGES))] * 4,
            *[sem((COLORS, STAGES))] * 2,
            *[sem((2, COLORS, STAGES))] * 2,
        ],
        compiler_params=pltpu.CompilerParams(
            vmem_limit_bytes=VMEM_LIMIT, collective_id=0, has_side_effects=True
        ),
        cost_estimate=pl.CostEstimate(
            flops=2 * n * n * n, bytes_accessed=300_000_000, transcendentals=0
        ),
        name="sweep_over_all_rows",
    )(phi, weights, labels.reshape(1, rows))
    return solution.reshape(padded, n), residual, delta


def body(inputs, labels, frequencies, phases, weights):
    groups = lax.axis_size("grp")
    width = frequencies.shape[1]
    classes = weights.shape[1]
    padded = -(-classes // 1024) * 1024
    scale = (2.0 / (groups * width)) ** 0.5
    swap = [(0, 1), (1, 0)]
    arg = (
        jnp.dot(inputs.astype(jnp.float32), frequencies, precision=lax.Precision.HIGHEST)
        + phases[None, :]
    )
    phi = (scale * jnp.cos(arg)).astype(jnp.bfloat16)
    solution, residual, delta = sweep_over_all_rows(phi, weights.T, labels, padded)
    step = DAMP * solution[:classes]
    half = padded // 2
    change = delta + lax.ppermute(delta, "grp", swap)
    return (
        weights + step.T,
        jnp.concatenate([residual[:, :half], residual[:, half:] - change], axis=1),
    )


def solution(mesh):
    return jax.shard_map(
        body,
        mesh=mesh,
        in_specs=(P("row", None), P("row"), P(None, "grp"), P("grp"), P("grp", None)),
        out_specs=(P("grp", None), P("row", None)),
        check_vma=False,
    )
```
